32 devices in a mesh: gx: 4 (over y, core), gy: 4 (over z), ha: 2 (over x).
Axes of the slice: x: 2, y: 2, z: 4, core: 2. Of those that a mesh axis runs over, the one named last changes fastest.
Arguments:
- value: float32 [4, 16, 32, 512], P(None, 'ha', 'gy', 'gx'), may hold values from -6 to 6
- obstacles: float32 [5, 128], replicated, may hold values from -1 to 1
- obstacle_slots: int32 [4, 16], P('ha'), may hold values from 0 to 127
- horizon: float32 [1], replicated, may hold values from 0.5 to 2
- speed_offset: int32 [1], replicated, may hold values from 2 to 11
Outputs:
- next_value: float32 [4, 16, 32, 512], P(None, 'ha', 'gy', 'gx')
The draws below stay inside these ranges and needn't reach their ends.
Inputs may be any that keep to these rules, and one draw needn't show every extreme that they name: `obstacle_slots`: each heading group of 4 headings lists 16 obstacle numbers, repeats allowed.
All inputs are finite; a program needn't handle non-finite values.
Results may differ from the reference program's by a relative error of at most 0.00002.
Values sent between devices are 32-bit elements; how exact they have to be, the bound alone decides.
No kernel may reach another device: no remote copies, remote signals or barrier semaphores. Data moves between devices by JAX's collectives and lax.ppermute only.
A program may use at most 64 MiB of HBM per device.

```python
import math
import jax
import jax.numpy as jnp
from jax import lax

NV = 4
GH = 4
SLOTS = 16
OBST = 128
NX = 512
NY = 32
NH = 16
GROUPS = 4


def with_ends(array, own_key, least, largest):
    dims = array.shape
    index_at = [jax.random.randint(jax.random.fold_in(own_key, axis), (), 0, dims[axis]) for axis in range(len(dims))]
    array = array.at[tuple(index_at)].set(least)
    longest = dims.index(max(dims))
    index_at[longest] = (index_at[longest] + 1) % dims[longest]
    return array.at[tuple(index_at)].set(largest)


def steps_of(key, dims, cuts, least, top_value):
    level, own = 1.0, jax.random.fold_in(key, 6)
    for axis_at, blocks in cuts:
        draws = jnp.exp(jax.random.uniform(jax.random.fold_in(own, axis_at), (blocks,), jnp.float32, least / len(cuts), top_value / len(cuts)))
        level = level * jnp.repeat(draws, dims[axis_at] // blocks).reshape([-1 if axis == axis_at else 1 for axis in range(len(dims))])
    return level


def scatter_about(own_key, dims, deviation, most, split=(), held_as=jnp.bfloat16):
    level = steps_of(own_key, dims, split, -0.22, 0.18) if split else 1.0
    result = jax.random.normal(own_key, dims, jnp.float32) * deviation * level
    return jnp.minimum(jnp.maximum(result, -most), most).astype(held_as)


def setup_inputs(seed: int = 0) -> dict:
    streams_of = jax.random.split(jax.random.key(seed), 6)
    value = scatter_about(streams_of[0], (NV, NH, NY, NX), 1.0, 6.0, ((1, 2), (2, 4), (3, 4)), jnp.float32)
    obstacles = jnp.clip(jax.random.uniform(streams_of[1], (5, OBST), jnp.float32, -1.0, 1.0), -1.0, 1.0)
    obstacle_slots = with_ends(jax.random.randint(streams_of[2], (GROUPS, SLOTS), 0, OBST), jax.random.fold_in(streams_of[2], 1), 0, OBST - 1).astype(jnp.int32)
    horizon = jnp.clip(jax.random.uniform(streams_of[3], (1,), jnp.float32, 0.5, 2.0), 0.5, 2.0)
    speed_offset = jax.random.randint(streams_of[4], (1,), 2, 12).astype(jnp.int32)
    return {"value": value, "obstacles": obstacles, "obstacle_slots": obstacle_slots, "horizon": horizon, "speed_offset": speed_offset}


cfl_number = 0.75
weno_eps = 1e-06
half_width = 20.0
speed_step = 0.5
turn_limit = 1.0
accel_limit = 4.0
obstacle_speed = 2.0
car_radius = 0.8
body_offsets = (-1.0, 0.0, 1.0)

def weno_side(outer_diff, middle_diff, inner_diff):
    weight_one = 1.0 / 3.0 / jnp.square(weno_eps + jnp.square(middle_diff - outer_diff))
    weight_two = 2.0 / 3.0 / jnp.square(weno_eps + jnp.square(inner_diff - middle_diff))
    return (weight_one * (1.5 * middle_diff - 0.5 * outer_diff) + weight_two * (0.5 * middle_diff + 0.5 * inner_diff)) / (weight_one + weight_two)

def slopes(padded, along_dim, spacing):
    length = padded.shape[along_dim] - 4
    samples = [lax.slice_in_dim(padded, offset_idx, offset_idx + length, axis=along_dim) for offset_idx in range(5)]
    back_far = (samples[1] - samples[0]) / spacing
    back_near = (samples[2] - samples[1]) / spacing
    ahead_near = (samples[3] - samples[2]) / spacing
    ahead_far = (samples[4] - samples[3]) / spacing
    return (weno_side(back_far, back_near, ahead_near), weno_side(ahead_far, ahead_near, back_near))

def hamiltonian_rate(pieces, speeds, angles, spreads, spacings):
    speed_minus, speed_plus = slopes(pieces[0], 0, spacings[0])
    head_minus, head_plus = slopes(pieces[1], 1, spacings[1])
    y_minus, y_plus = slopes(pieces[2], 2, spacings[2])
    x_minus, x_plus = slopes(pieces[3], 3, spacings[3])
    along_x = speeds[:, None, None, None] * jnp.cos(angles)[None, :, None, None]
    along_y = speeds[:, None, None, None] * jnp.sin(angles)[None, :, None, None]
    hamilton = along_x * (0.5 * (x_minus + x_plus)) + along_y * (0.5 * (y_minus + y_plus))
    hamilton = hamilton + turn_limit * jnp.abs(0.5 * (head_minus + head_plus)) + accel_limit * jnp.abs(0.5 * (speed_minus + speed_plus))
    damping = spreads[0] * (x_plus - x_minus) + spreads[1] * (y_plus - y_minus)
    damping = damping + turn_limit * (head_plus - head_minus) + accel_limit * (speed_plus - speed_minus)
    return jnp.minimum(0.0, hamilton - 0.5 * damping)

def speed_bounds(speeds, angles, step_x, step_y):
    along_x = jnp.abs(speeds[:, None] * jnp.cos(angles)[None, :])
    along_y = jnp.abs(speeds[:, None] * jnp.sin(angles)[None, :])
    return (jnp.max(along_x), jnp.max(along_y), jnp.max(along_x / step_x + along_y / step_y))

def group_field(obstacles, horizon, step_time, x_cells, y_cells, angle_group, slot_row):
    moment = horizon[0] + step_time
    centre_x = half_width * obstacles[0] + moment * (obstacle_speed * obstacles[2])
    centre_y = half_width * obstacles[1] + moment * (obstacle_speed * obstacles[3])
    reach = 1.25 + 0.75 * obstacles[4] + car_radius
    centre_x = jnp.take(centre_x, slot_row)[None, :, None, None]
    centre_y = jnp.take(centre_y, slot_row)[None, :, None, None]
    reach = jnp.take(reach, slot_row)[None, :, None, None]
    cosine = jnp.cos(angle_group)[:, None, None, None]
    sine = jnp.sin(angle_group)[:, None, None, None]
    nearest = None
    for offset in body_offsets:
        moved_x = x_cells[None, None, None, :] + offset * cosine
        moved_y = y_cells[None, None, :, None] + offset * sine
        clearance = jnp.sqrt(jnp.square(moved_x - centre_x) + jnp.square(moved_y - centre_y)) - reach
        closest = lax.optimization_barrier(jnp.min(clearance, axis=1))
        nearest = closest if nearest is None else jnp.minimum(nearest, closest)
    return nearest

def advance(surface, time_step, speeds, angles, spreads, spacings):
    pieces = (jnp.pad(surface, ((2, 2), (0, 0), (0, 0), (0, 0)), mode='edge'), jnp.pad(surface, ((0, 0), (2, 2), (0, 0), (0, 0)), mode='wrap'), jnp.pad(surface, ((0, 0), (0, 0), (2, 2), (0, 0)), mode='edge'), jnp.pad(surface, ((0, 0), (0, 0), (0, 0), (2, 2)), mode='edge'))
    return surface + time_step * hamiltonian_rate(pieces, speeds, angles, spreads, spacings)

def reference(value, obstacles, obstacle_slots, horizon, speed_offset):
    step_x = 2.0 * half_width / NX
    step_y = 2.0 * half_width / NY
    step_h = 2.0 * math.pi / NH
    speeds = speed_step * (speed_offset.astype(jnp.float32)[0] + jnp.arange(NV, dtype=jnp.float32))
    angles = jnp.arange(NH, dtype=jnp.int32).astype(jnp.float32) * step_h - math.pi
    spread_x, spread_y, fastest = speed_bounds(speeds, angles, step_x, step_y)
    rate_total = fastest + turn_limit / step_h + accel_limit / speed_step
    time_step = cfl_number / rate_total
    spacings = (speed_step, step_h, step_y, step_x)
    section_one = advance(value, time_step, speeds, angles, (spread_x, spread_y), spacings)
    section_two = advance(section_one, time_step, speeds, angles, (spread_x, spread_y), spacings)
    x_cells = (jnp.arange(NX, dtype=jnp.int32).astype(jnp.float32) + 0.5) * step_x - half_width
    y_cells = (jnp.arange(NY, dtype=jnp.int32).astype(jnp.float32) + 0.5) * step_y - half_width

    def one_group(packed):
        return group_field(obstacles, horizon, time_step, x_cells, y_cells, packed[0], packed[1])
    failure = lax.map(one_group, (angles.reshape(NH // GH, GH), obstacle_slots))
    failure = failure.reshape(NH, NY, NX)
    return jnp.minimum(0.5 * (value + section_two), failure[None])
```

```python
import functools
import math

import jax
import jax.numpy as jnp
import numpy as np
from jax import lax
from jax.experimental import pallas as pl
from jax.experimental.pallas import tpu as pltpu
from jax.sharding import PartitionSpec as P

GH = 4

cfl_number = 0.75
weno_eps = 1e-06
half_width = 20.0
speed_step = 0.5
turn_limit = 1.0
accel_limit = 4.0
obstacle_speed = 2.0
car_radius = 0.8

DEPTH = 4
SLOT = 2 * DEPTH


class Plan:
    def __init__(self, mesh, shape):
        self.speeds, self.heads, self.rows, self.cols = shape
        self.axes = dict(mesh.shape)
        self.total_heads = self.heads * self.axes["ha"]
        self.step_x = 2.0 * half_width / (self.cols * self.axes["gx"])
        self.step_y = 2.0 * half_width / (self.rows * self.axes["gy"])
        self.step_h = 2.0 * math.pi / self.total_heads
        assert self.rows == 2 * DEPTH and self.heads >= DEPTH and self.heads % GH == 0
        assert SLOT * (self.heads + DEPTH) <= self.cols
        assert all(size % 2 == 0 for size in self.axes.values())
        index = np.arange(self.total_heads, dtype=np.float32)
        angles = index * np.float32(self.step_h) - np.float32(math.pi)
        self.cosines = np.cos(angles.astype(np.float64))
        self.sines = np.sin(angles.astype(np.float64))
        self.most_cos = float(np.max(np.abs(self.cosines)))
        self.most_sin = float(np.max(np.abs(self.sines)))
        self.most_rate = float(
            np.max(np.abs(self.cosines) / self.step_x + np.abs(self.sines) / self.step_y)
        )

    def trig(self, head):
        place = lax.axis_index("ha")
        picked = []
        for table in (self.cosines, self.sines):
            values = [
                float(table[(a * self.heads + head) % self.total_heads])
                for a in range(self.axes["ha"])
            ]
            value = jnp.float32(values[0])
            for a in range(1, len(values)):
                value = jnp.where(place == a, jnp.float32(values[a]), value)
            picked.append(value)
        return picked

    def pace(self, offset_ref):
        base = offset_ref[0].astype(jnp.float32)
        speeds = [speed_step * (base + float(k)) for k in range(self.speeds)]
        top = functools.reduce(jnp.maximum, [jnp.abs(speed) for speed in speeds])
        total = top * self.most_rate + (turn_limit / self.step_h + accel_limit / speed_step)
        time_step = cfl_number / jnp.full((self.rows, self.cols), total, jnp.float32)
        return speeds, (top * self.most_cos, top * self.most_sin), time_step


def partners(axis, odd, wrap):
    count = lax.axis_size(axis)
    pairs = []
    for i in range(1 if odd else 0, count, 2):
        j = i + 1
        if j < count or wrap:
            pairs += [(i, j % count), (j % count, i)]
    return pairs


def swap(payload, axis, odd, wrap=False):
    return lax.ppermute(payload, axis, partners(axis, odd, wrap))


def by_side(axis, even_block, odd_block):
    is_even = lax.axis_index(axis) % 2 == 0
    return jnp.where(is_even, odd_block, even_block), jnp.where(is_even, even_block, odd_block)


def is_first(axis):
    return lax.axis_index(axis) == 0


def is_last(axis):
    return lax.axis_index(axis) == lax.axis_size(axis) - 1


def call(body, plan, out_shapes, args, specs, scratch=(), flops=1000000):
    space = {"v": pltpu.VMEM, "s": pltpu.SMEM}
    return pl.pallas_call(
        functools.partial(body, plan),
        out_shape=[jax.ShapeDtypeStruct(shape, jnp.float32) for shape in out_shapes],
        in_specs=[pl.BlockSpec(memory_space=space[s]) for s in specs],
        out_specs=[pl.BlockSpec(memory_space=pltpu.VMEM) for _ in out_shapes],
        scratch_shapes=scratch,
        name=body.__name__,
        cost_estimate=pl.CostEstimate(flops=flops, bytes_accessed=400000, transcendentals=0),
    )(*args)


def iota(plan, dim):
    return lax.broadcasted_iota(jnp.int32, (plan.rows, plan.cols), dim)


def pack_rows(plan, value, even_out, odd_out):
    row = iota(plan, 0)
    is_even = lax.axis_index("gy") % 2 == 0
    for v in range(plan.speeds):
        for pair in range(plan.heads // 2):
            one, two = value[v, 2 * pair], value[v, 2 * pair + 1]
            low = jnp.where(row < DEPTH, one, pltpu.roll(two, DEPTH, 0))
            high = jnp.where(row < DEPTH, pltpu.roll(one, DEPTH, 0), two)
            even_out[v, pair] = jnp.where(is_even, high, low)
            odd_out[v, pair] = jnp.where(is_even, low, high)


def unpack_rows(plan, value, even_in, odd_in, ring_out, corner_out):
    row = iota(plan, 0)
    at_first = jnp.logical_and(row >= DEPTH, is_first("gy"))
    at_last = jnp.logical_and(row < DEPTH, is_last("gy"))
    inner = jnp.logical_or(row < 2, row >= plan.rows - 2)
    edge_heads = (0, 1, plan.heads - 2, plan.heads - 1)
    for v in range(plan.speeds):
        kept = {}
        for pair in range(plan.heads // 2):
            before, after = by_side("gy", even_in[v, pair], odd_in[v, pair])
            one = jnp.where(row < DEPTH, after, pltpu.roll(before, DEPTH, 0))
            two = jnp.where(row < DEPTH, pltpu.roll(after, DEPTH, 0), before)
            for h, ring in ((2 * pair, one), (2 * pair + 1, two)):
                ring = clamp_rows(plan, value[v, h], ring, at_first, at_last)
                ring_out[v, h] = ring
                kept[h] = ring
        for side in range(2):
            one, two = kept[edge_heads[2 * side]], kept[edge_heads[2 * side + 1]]
            corner_out[v, side] = jnp.where(inner, one, pltpu.roll(two, DEPTH, 0))


def clamp_rows(plan, own, ring, at_first, at_last):
    shape = (plan.rows, plan.cols)
    ring = jnp.where(at_first, jnp.broadcast_to(own[0:1], shape), ring)
    return jnp.where(at_last, jnp.broadcast_to(own[plan.rows - 1 :], shape), ring)


def clamp_cols(plan, own, ring, at_first, at_last):
    shape = (plan.rows, plan.cols)
    ring = jnp.where(at_first, jnp.broadcast_to(own[:, 0:1], shape), ring)
    return jnp.where(at_last, jnp.broadcast_to(own[:, plan.cols - 1 :], shape), ring)


def pack_cols(plan, value, heads_even, heads_odd, ring, packed_out):
    slot_id = iota(plan, 1) // SLOT
    for v in range(plan.speeds):
        packed = jnp.zeros((plan.rows, plan.cols), jnp.float32)
        for h in range(-2, plan.heads + 2):
            block = head_block(plan, value, heads_even, heads_odd, v, h)
            slot = h + 2
            packed = jnp.where(slot_id == slot, pltpu.roll(block, DEPTH + SLOT * slot, 1), packed)
        packed_out[v, 0] = packed
        packed = jnp.zeros((plan.rows, plan.cols), jnp.float32)
        for h in range(plan.heads):
            slot = h + 2
            moved = pltpu.roll(ring[v, h], DEPTH + SLOT * slot, 1)
            packed = jnp.where(slot_id == slot, moved, packed)
        packed_out[v, 1] = packed


def head_block(plan, value, heads_even, heads_odd, v, h):
    if 0 <= h < plan.heads:
        return value[v, h]
    source = h % plan.heads
    if heads_odd is None:
        return heads_even[v, source]
    sides = by_side("ha", heads_even[v, source], heads_odd[v, source])
    return sides[0] if h < 0 else sides[1]


def failure_field(plan, obstacles, slots, horizon, offset, failure_out):
    _, _, time_step = plan.pace(offset)
    moment = horizon[0] + time_step
    col = (lax.axis_index("gx") * plan.cols + iota(plan, 1)).astype(jnp.float32)
    row = (lax.axis_index("gy") * plan.rows + iota(plan, 0)).astype(jnp.float32)
    x_cells = (col + 0.5) * plan.step_x - half_width
    y_cells = (row + 0.5) * plan.step_y - half_width
    for group in range(plan.heads // GH):
        angles = [plan.trig(group * GH + g) for g in range(GH)]

        def step(slot, nearest):
            which = slots[group, slot]
            centre_x = half_width * obstacles[0, which]
            centre_y = half_width * obstacles[1, which]
            away_x = x_cells - (centre_x + moment * (obstacle_speed * obstacles[2, which]))
            away_y = y_cells - (centre_y + moment * (obstacle_speed * obstacles[3, which]))
            reach = 1.25 + 0.75 * obstacles[4, which] + car_radius
            middle = away_x * away_x + away_y * away_y
            updated = []
            for g in range(GH):
                cosine, sine = angles[g]
                front_x, front_y = away_x + cosine, away_y + sine
                back_x, back_y = away_x - cosine, away_y - sine
                squared = jnp.minimum(
                    middle,
                    jnp.minimum(
                        front_x * front_x + front_y * front_y, back_x * back_x + back_y * back_y
                    ),
                )
                updated.append(jnp.minimum(nearest[g], jnp.sqrt(squared) - reach))
            return tuple(updated)

        far = jnp.full((plan.rows, plan.cols), 1e30, jnp.float32)
        nearest = lax.fori_loop(0, slots.shape[1], step, (far,) * GH, unroll=2)
        for g in range(GH):
            failure_out[group * GH + g] = nearest[g]


def sharp(bend, floor):
    t = bend * bend + floor
    return t * t


def sides_of(bends, floor):
    before, here, after = bends
    half = 0.5 * sharp(here, floor)
    low = half + sharp(before, floor)
    high = half + sharp(after, floor)
    return (before - here) * high, (after - here) * low, half / (low * high)


def bends_of(samples):
    steps = [samples[i + 1] - samples[i] for i in range(4)]
    return [steps[i + 1] - steps[i] for i in range(3)], samples[3] - samples[1]


def drift_term(samples, floor, drift, spread, spacing):
    bends, across = bends_of(samples)
    a, b, r = sides_of(bends, floor)
    quarter = 0.25 / spacing
    return (drift * (0.5 / spacing)) * across + r * (
        ((spread + drift) * quarter) * a + ((spread - drift) * quarter) * b
    )


def limit_term(bends, across, floor, limit, spacing):
    a, b, r = sides_of(bends, floor)
    r = r * (0.25 * limit / spacing)
    return jnp.abs((0.5 * limit / spacing) * across + r * (a - b)) + r * (a + b)


def ring_samples(block, ring, place, axis, length):
    return [
        pltpu.roll(jnp.where(place >= length - 2, ring, block), 2, axis),
        pltpu.roll(jnp.where(place >= length - 1, ring, block), 1, axis),
        block,
        pltpu.roll(jnp.where(place < 1, ring, block), length - 1, axis),
        pltpu.roll(jnp.where(place < 2, ring, block), length - 2, axis),
    ]


def speed_terms(plan, blocks):
    floor = weno_eps * speed_step * speed_step
    count = len(blocks)
    at = lambda k: blocks[min(max(k, 0), count - 1)]
    steps = {k: at(k + 1) - at(k) for k in range(0, count - 1)}
    zero = jnp.zeros_like(blocks[0])
    step = lambda k: steps.get(k, zero)
    terms = []
    for k in range(count):
        bends = [step(k + j) - step(k + j - 1) for j in (-1, 0, 1)]
        terms.append(limit_term(bends, at(k + 1) - at(k - 1), floor, accel_limit, speed_step))
    return terms


def advanced(plan, blocks, row_samples, col_samples, head_samples, pace, trig):
    speeds, spreads, time_step = pace
    terms = speed_terms(plan, blocks)
    results = []
    for v, block in enumerate(blocks):
        bends, across = bends_of(head_samples[v])
        rate = terms[v] + limit_term(
            bends, across, weno_eps * plan.step_h**2, turn_limit, plan.step_h
        )
        rate = rate + drift_term(
            row_samples[v], weno_eps * plan.step_y**2, speeds[v] * trig[1], spreads[1], plan.step_y
        )
        rate = rate + drift_term(
            col_samples[v], weno_eps * plan.step_x**2, speeds[v] * trig[0], spreads[0], plan.step_x
        )
        results.append(block + time_step * jnp.minimum(rate, 0.0))
    return results


def step_kernel(plan, *refs):
    wide = plan.axes["ha"] > 2
    names = ["value", "heads_even"] + (["heads_odd"] if wide else [])
    names += ["ring", "corner_even"] + (["corner_odd"] if wide else [])
    names += ["packed", "cols_even", "cols_odd", "failure", "offset", "out"]
    names += ["f_a", "f_b", "x_a", "x_b", "s_a", "s_b", "x_s", "trig"]
    r = dict(zip(names, refs, strict=True))
    nv, heads, rows, cols = plan.speeds, plan.heads, plan.rows, plan.cols
    heads_odd, corner_odd = r.get("heads_odd"), r.get("corner_odd")
    pace = plan.pace(r["offset"])
    row, col = iota(plan, 0), iota(plan, 1)
    lower = col % SLOT < DEPTH
    row_first = jnp.logical_and(row >= DEPTH, is_first("gy"))
    row_last = jnp.logical_and(row < DEPTH, is_last("gy"))
    col_first = jnp.logical_and(col >= cols // 2, is_first("gx"))
    col_last = jnp.logical_and(col < cols // 2, is_last("gx"))
    f_a, f_b, x_a, x_b = r["f_a"], r["f_b"], r["x_a"], r["x_b"]
    s_a, s_b, x_s = r["s_a"], r["s_b"], r["x_s"]

    cos_lanes = jnp.zeros((rows, cols), jnp.float32)
    sin_lanes = jnp.zeros((rows, cols), jnp.float32)
    for h in range(-2, heads + 2):
        cosine, sine = plan.trig(h)
        r["trig"][0, h + 2] = cosine
        r["trig"][1, h + 2] = sine
        cos_lanes = jnp.where(col // SLOT == h + 2, cosine, cos_lanes)
        sin_lanes = jnp.where(col // SLOT == h + 2, sine, sin_lanes)

    around = []
    for v in range(nv):
        for h in range(-DEPTH, heads + DEPTH):
            f_a[v, h + DEPTH] = head_block(plan, r["value"], r["heads_even"], heads_odd, v, h)
        for h in range(heads):
            f_b[v, h + 2] = r["ring"][v, h]
        for side in range(2):
            tile = r["corner_even"][v, 1 - side]
            if corner_odd is not None:
                tile = by_side("ha", tile, corner_odd[v, 1 - side])[side]
            base = heads + 2 if side else 0
            f_b[v, base] = tile
            f_b[v, base + 1] = pltpu.roll(tile, DEPTH, 0)
        pair = []
        for part in range(2):
            before, after = by_side("gx", r["cols_even"][v, part], r["cols_odd"][v, part])
            pair.append(jnp.where(lower, before, after))
        around.append(pair)
        for h in range(-2, heads + 2):
            slot = h + 2
            ring = pltpu.roll(pair[0], cols - DEPTH - SLOT * slot, 1)
            x_a[v, slot] = clamp_cols(plan, f_a[v, h + DEPTH], ring, col_first, col_last)
        for h in range(heads):
            slot = h + 2
            ring = pltpu.roll(pair[1], cols - DEPTH - SLOT * slot, 1)
            x_b[v, h] = clamp_cols(plan, f_b[v, slot], ring, col_first, col_last)

    def block_step(h, main, ring, row_of, x_of, base, store):
        blocks = [main[v, h + base] for v in range(nv)]
        heads_near = [[main[v, h + base + j] for j in range(-2, 3)] for v in range(nv)]
        rows_near = [
            ring_samples(blocks[v], ring[v, row_of(h)], row, 0, rows) for v in range(nv)
        ]
        cols_near = [ring_samples(blocks[v], x_of(v, h), col, 1, cols) for v in range(nv)]
        trig = (r["trig"][0, h + 2], r["trig"][1, h + 2])
        results = advanced(plan, blocks, rows_near, cols_near, heads_near, pace, trig)
        for v in range(nv):
            store(v, h, results[v])

    def put_a(v, h, block):
        s_a[v, h + 2] = block

    def put_b(v, h, block):
        s_b[v, h] = block

    def first_a(i, carry):
        block_step(i - 2, f_a, f_b, lambda h: h + 2, lambda v, h: x_a[v, h + 2], DEPTH, put_a)
        return carry

    def first_b(h, carry):
        block_step(h, f_b, f_a, lambda h: h + DEPTH, lambda v, h: x_b[v, h], 2, put_b)
        return carry

    lax.fori_loop(0, heads + 4, first_a, 0)
    lax.fori_loop(0, heads, first_b, 0)

    faces = []
    for keep_own in (jnp.logical_not(lower), lower):
        mains = [jnp.where(keep_own, r["packed"][v, 0], around[v][0]) for v in range(nv)]
        rings = [jnp.where(keep_own, r["packed"][v, 1], around[v][1]) for v in range(nv)]
        rows_near = [ring_samples(mains[v], rings[v], row, 0, rows) for v in range(nv)]
        shift = lambda block, lanes: pltpu.roll(block, lanes % cols, 1)
        cols_near = [[shift(mains[v], -j) for j in (-2, -1)] + [mains[v]] for v in range(nv)]
        cols_near = [near + [shift(near[2], -j) for j in (1, 2)] for near in cols_near]
        heads_near = [
            [mains[v] if j == 0 else shift(mains[v], -SLOT * j) for j in range(-2, 3)]
            for v in range(nv)
        ]
        trig = (cos_lanes, sin_lanes)
        faces.append(advanced(plan, mains, rows_near, cols_near, heads_near, pace, trig))

    for v in range(nv):
        both = jnp.where(lower, faces[0][v], faces[1][v])
        for h in range(heads):
            own = s_a[v, h + 2]
            ring = pltpu.roll(both, cols - DEPTH - SLOT * (h + 2), 1)
            x_s[v, h] = clamp_cols(plan, own, ring, col_first, col_last)
            s_b[v, h] = clamp_rows(plan, own, s_b[v, h], row_first, row_last)

    def put_out(v, h, block):
        half = 0.5 * (r["value"][v, h] + block)
        r["out"][v, h] = jnp.minimum(half, r["failure"][h])

    def second(h, carry):
        block_step(h, s_a, s_b, lambda h: h, lambda v, h: x_s[v, h], 2, put_out)
        return carry

    lax.fori_loop(0, heads, second, 0)


def local(plan, value, obstacles, obstacle_slots, horizon, speed_offset):
    nv, heads, rows, cols = value.shape
    wide = plan.axes["ha"] > 2
    tile = (rows, cols)

    def turn_swaps(payload):
        blocks = [swap(payload, "ha", False, True)]
        return blocks + [swap(payload, "ha", True, True)] if wide else blocks

    beside = turn_swaps(value)
    half = (nv, heads // 2) + tile
    even_rows, odd_rows = call(pack_rows, plan, [half, half], [value], "v")
    even_rows = swap(even_rows, "gy", False)
    odd_rows = swap(odd_rows, "gy", True)
    (failure,) = call(
        failure_field,
        plan,
        [(heads,) + tile],
        [obstacles, obstacle_slots, horizon, speed_offset],
        "ssss",
    )
    ring, corner = call(
        unpack_rows, plan, [value.shape, (nv, 2) + tile], [value, even_rows, odd_rows], "vvv"
    )
    corners = turn_swaps(corner)
    pack = pack_cols if wide else pack_cols_narrow
    (packed,) = call(
        pack, plan, [(nv, 2) + tile], [value, *beside, ring], "v" * (2 + len(beside))
    )
    even_cols = swap(packed, "gx", False)
    odd_cols = swap(packed, "gx", True)
    args = [value, *beside, ring, *corners, packed, even_cols, odd_cols, failure]
    scratch = [
        pltpu.VMEM((nv, heads + 2 * DEPTH) + tile, jnp.float32),
        pltpu.VMEM((nv, heads + 4) + tile, jnp.float32),
        pltpu.VMEM((nv, heads + 4) + tile, jnp.float32),
        pltpu.VMEM((nv, heads) + tile, jnp.float32),
        pltpu.VMEM((nv, heads + 4) + tile, jnp.float32),
        pltpu.VMEM((nv, heads) + tile, jnp.float32),
        pltpu.VMEM((nv, heads) + tile, jnp.float32),
        pltpu.SMEM((2, heads + 4), jnp.float32),
    ]
    (out,) = call(
        step_kernel,
        plan,
        [value.shape],
        args + [speed_offset],
        "v" * len(args) + "s",
        scratch,
        flops=100000000,
    )
    return out


def pack_cols_narrow(plan, value, heads_even, ring, packed_out):
    pack_cols(plan, value, heads_even, None, ring, packed_out)


def solution(mesh):
    in_specs = (P(None, "ha", "gy", "gx"), P(), P("ha", None), P(), P())
    out_specs = P(None, "ha", "gy", "gx")

    def body(value, *rest):
        return local(Plan(mesh, value.shape), value, *rest)

    return jax.shard_map(body, mesh=mesh, in_specs=in_specs, out_specs=out_specs, check_vma=False)
```

```python
import functools
import math

import jax
import jax.numpy as jnp
import numpy as np
from jax import lax
from jax.experimental import pallas as pl
from jax.experimental.pallas import tpu as pltpu
from jax.sharding import PartitionSpec as P

GH = 4

cfl_number = 0.75
weno_eps = 1e-06
half_width = 20.0
speed_step = 0.5
turn_limit = 1.0
accel_limit = 4.0
obstacle_speed = 2.0
car_radius = 0.8

DEPTH = 4
SLOT = 2 * DEPTH


class Plan:
    def __init__(self, mesh, shape):
        self.speeds, self.heads, self.rows, self.cols = shape
        self.axes = dict(mesh.shape)
        self.total_heads = self.heads * self.axes["ha"]
        self.step_x = 2.0 * half_width / (self.cols * self.axes["gx"])
        self.step_y = 2.0 * half_width / (self.rows * self.axes["gy"])
        self.step_h = 2.0 * math.pi / self.total_heads
        assert self.rows == 2 * DEPTH and self.heads >= DEPTH and self.heads % GH == 0
        assert SLOT * (self.heads + DEPTH) <= self.cols
        assert all(size % 2 == 0 for size in self.axes.values())
        index = np.arange(self.total_heads, dtype=np.float32)
        angles = index * np.float32(self.step_h) - np.float32(math.pi)
        self.cosines = np.cos(angles.astype(np.float64))
        self.sines = np.sin(angles.astype(np.float64))
        self.most_cos = float(np.max(np.abs(self.cosines)))
        self.most_sin = float(np.max(np.abs(self.sines)))
        self.most_rate = float(
            np.max(np.abs(self.cosines) / self.step_x + np.abs(self.sines) / self.step_y)
        )

    def trig(self, head):
        place = lax.axis_index("ha")
        picked = []
        for table in (self.cosines, self.sines):
            values = [
                float(table[(a * self.heads + head) % self.total_heads])
                for a in range(self.axes["ha"])
            ]
            value = jnp.float32(values[0])
            for a in range(1, len(values)):
                value = jnp.where(place == a, jnp.float32(values[a]), value)
            picked.append(value)
        return picked

    def pace(self, offset_ref):
        base = offset_ref[0].astype(jnp.float32)
        speeds = [speed_step * (base + float(k)) for k in range(self.speeds)]
        top = functools.reduce(jnp.maximum, [jnp.abs(speed) for speed in speeds])
        total = top * self.most_rate + (turn_limit / self.step_h + accel_limit / speed_step)
        time_step = cfl_number / jnp.full((self.rows, self.cols), total, jnp.float32)
        return speeds, (top * self.most_cos, top * self.most_sin), time_step


def swap(payload, axis, odd, wrap=False):
    count = lax.axis_size(axis)
    if axis != "gy" or not odd or wrap:
        first = 1 if odd else 0
        pairs = [(i, (i + 1) % count) for i in range(first, count, 2)]
        return lax.ppermute(payload, axis, pairs + [(j, i) for i, j in pairs])
    pairs = []
    for x in range(lax.axis_size("gx")):
        for y in range(count):
            end = y in (0, count - 1)
            there = (x ^ 1, y) if end else (x, y + 1 if y % 2 else y - 1)
            pairs.append((x * count + y, there[0] * count + there[1]))
    return lax.ppermute(payload, ("gx", axis), pairs)


def by_side(axis, even_block, odd_block):
    is_even = lax.axis_index(axis) % 2 == 0
    return jnp.where(is_even, odd_block, even_block), jnp.where(is_even, even_block, odd_block)


def is_first(axis):
    return lax.axis_index(axis) == 0


def is_last(axis):
    return lax.axis_index(axis) == lax.axis_size(axis) - 1


def call(body, plan, out_shapes, args, specs, scratch=(), flops=1000000):
    space = {"v": pltpu.VMEM, "s": pltpu.SMEM, "a": pl.ANY}
    return pl.pallas_call(
        functools.partial(body, plan),
        out_shape=[jax.ShapeDtypeStruct(shape, jnp.float32) for shape in out_shapes],
        in_specs=[pl.BlockSpec(memory_space=space[s]) for s in specs],
        out_specs=[pl.BlockSpec(memory_space=pltpu.VMEM) for _ in out_shapes],
        scratch_shapes=scratch,
        name=body.__name__,
        cost_estimate=pl.CostEstimate(flops=flops, bytes_accessed=400000, transcendentals=0),
        compiler_params=pltpu.CompilerParams(vmem_limit_bytes=8 * 2**20),
    )(*args)


def iota(plan, dim):
    return lax.broadcasted_iota(jnp.int32, (plan.rows, plan.cols), dim)


def pack_rows(plan, value, even_out, odd_out):
    row = iota(plan, 0)
    is_even = lax.axis_index("gy") % 2 == 0
    for v in range(plan.speeds):
        for pair in range(plan.heads // 2):
            one, two = value[v, 2 * pair], value[v, 2 * pair + 1]
            low = jnp.where(row < DEPTH, one, pltpu.roll(two, DEPTH, 0))
            high = jnp.where(row < DEPTH, pltpu.roll(one, DEPTH, 0), two)
            even_out[v, pair] = jnp.where(is_even, high, low)
            odd_out[v, pair] = jnp.where(is_even, low, high)


def unpack_rows(plan, value, even_in, odd_in, _, ring_out, corner_out):
    row = iota(plan, 0)
    at_first = jnp.logical_and(row >= DEPTH, is_first("gy"))
    at_last = jnp.logical_and(row < DEPTH, is_last("gy"))
    inner = jnp.logical_or(row < 2, row >= plan.rows - 2)
    edge_heads = (0, 1, plan.heads - 2, plan.heads - 1)
    for v in range(plan.speeds):
        kept = {}
        for pair in range(plan.heads // 2):
            before, after = by_side("gy", even_in[v, pair], odd_in[v, pair])
            one = jnp.where(row < DEPTH, after, pltpu.roll(before, DEPTH, 0))
            two = jnp.where(row < DEPTH, pltpu.roll(after, DEPTH, 0), before)
            for h, ring in ((2 * pair, one), (2 * pair + 1, two)):
                ring = clamp_rows(plan, value[v, h], ring, at_first, at_last)
                ring_out[v, h] = ring
                kept[h] = ring
        for side in range(2):
            one, two = kept[edge_heads[2 * side]], kept[edge_heads[2 * side + 1]]
            corner_out[v, side] = jnp.where(inner, one, pltpu.roll(two, DEPTH, 0))


def clamp_rows(plan, own, ring, at_first, at_last):
    shape = (plan.rows, plan.cols)
    ring = jnp.where(at_first, jnp.broadcast_to(own[0:1], shape), ring)
    return jnp.where(at_last, jnp.broadcast_to(own[plan.rows - 1 :], shape), ring)


def clamp_cols(plan, own, ring, at_first, at_last):
    shape = (plan.rows, plan.cols)
    ring = jnp.where(at_first, jnp.broadcast_to(own[:, 0:1], shape), ring)
    return jnp.where(at_last, jnp.broadcast_to(own[:, plan.cols - 1 :], shape), ring)


def pack_cols(plan, value, heads_even, heads_odd, ring, packed_out):
    slot_id = iota(plan, 1) // SLOT
    for v in range(plan.speeds):
        packed = jnp.zeros((plan.rows, plan.cols), jnp.float32)
        for h in range(-2, plan.heads + 2):
            block = head_block(plan, value, heads_even, heads_odd, v, h)
            slot = h + 2
            packed = jnp.where(slot_id == slot, pltpu.roll(block, DEPTH + SLOT * slot, 1), packed)
        packed_out[v, 0] = packed
        packed = jnp.zeros((plan.rows, plan.cols), jnp.float32)
        for h in range(plan.heads):
            slot = h + 2
            moved = pltpu.roll(ring[v, h], DEPTH + SLOT * slot, 1)
            packed = jnp.where(slot_id == slot, moved, packed)
        packed_out[v, 1] = packed


def head_block(plan, value, heads_even, heads_odd, v, h):
    if 0 <= h < plan.heads:
        return value[v, h]
    source = h % plan.heads
    if heads_odd is None:
        return heads_even[v, source]
    sides = by_side("ha", heads_even[v, source], heads_odd[v, source])
    return sides[0] if h < 0 else sides[1]


def failure_field(plan, obstacles, slots, horizon, offset, failure_out):
    _, _, time_step = plan.pace(offset)
    moment = horizon[0] + time_step
    col = (lax.axis_index("gx") * plan.cols + iota(plan, 1)).astype(jnp.float32)
    row = (lax.axis_index("gy") * plan.rows + iota(plan, 0)).astype(jnp.float32)
    x_cells = (col + 0.5) * plan.step_x - half_width
    y_cells = (row + 0.5) * plan.step_y - half_width
    for group in range(plan.heads // GH):
        angles = [plan.trig(group * GH + g) for g in range(GH)]

        def step(slot, nearest):
            which = slots[group, slot]
            centre_x = half_width * obstacles[0, which]
            centre_y = half_width * obstacles[1, which]
            away_x = x_cells - (centre_x + moment * (obstacle_speed * obstacles[2, which]))
            away_y = y_cells - (centre_y + moment * (obstacle_speed * obstacles[3, which]))
            reach = 1.25 + 0.75 * obstacles[4, which] + car_radius
            middle = away_x * away_x + away_y * away_y
            updated = []
            for g in range(GH):
                cosine, sine = angles[g]
                front_x, front_y = away_x + cosine, away_y + sine
                back_x, back_y = away_x - cosine, away_y - sine
                squared = jnp.minimum(
                    middle,
                    jnp.minimum(
                        front_x * front_x + front_y * front_y, back_x * back_x + back_y * back_y
                    ),
                )
                updated.append(jnp.minimum(nearest[g], jnp.sqrt(squared) - reach))
            return tuple(updated)

        far = jnp.full((plan.rows, plan.cols), 1e30, jnp.float32)
        nearest = lax.fori_loop(0, slots.shape[1], step, (far,) * GH, unroll=2)
        for g in range(GH):
            failure_out[group * GH + g] = nearest[g]


def sharp(bend, floor):
    t = bend * bend + floor
    return t * t


def sides_of(bends, floor):
    before, here, after = bends
    half = 0.5 * sharp(here, floor)
    low = half + sharp(before, floor)
    high = half + sharp(after, floor)
    return (before - here) * high, (after - here) * low, half / (low * high)


def bends_of(samples):
    steps = [samples[i + 1] - samples[i] for i in range(4)]
    return [steps[i + 1] - steps[i] for i in range(3)], samples[3] - samples[1]


def drift_term(samples, floor, drift, spread, spacing):
    bends, across = bends_of(samples)
    a, b, r = sides_of(bends, floor)
    quarter = 0.25 / spacing
    return (drift * (0.5 / spacing)) * across + r * (
        ((spread + drift) * quarter) * a + ((spread - drift) * quarter) * b
    )


def limit_term(bends, across, floor, limit, spacing):
    a, b, r = sides_of(bends, floor)
    r = r * (0.25 * limit / spacing)
    return jnp.abs((0.5 * limit / spacing) * across + r * (a - b)) + r * (a + b)


def ring_samples(block, ring, place, axis, length):
    return [
        pltpu.roll(jnp.where(place >= length - 2, ring, block), 2, axis),
        pltpu.roll(jnp.where(place >= length - 1, ring, block), 1, axis),
        block,
        pltpu.roll(jnp.where(place < 1, ring, block), length - 1, axis),
        pltpu.roll(jnp.where(place < 2, ring, block), length - 2, axis),
    ]


def speed_terms(plan, blocks):
    floor = weno_eps * speed_step * speed_step
    count = len(blocks)
    at = lambda k: blocks[min(max(k, 0), count - 1)]
    steps = {k: at(k + 1) - at(k) for k in range(0, count - 1)}
    zero = jnp.zeros_like(blocks[0])
    step = lambda k: steps.get(k, zero)
    terms = []
    for k in range(count):
        bends = [step(k + j) - step(k + j - 1) for j in (-1, 0, 1)]
        terms.append(limit_term(bends, at(k + 1) - at(k - 1), floor, accel_limit, speed_step))
    return terms


def advanced(plan, blocks, row_samples, col_samples, head_samples, pace, trig):
    speeds, spreads, time_step = pace
    terms = speed_terms(plan, blocks)
    results = []
    for v, block in enumerate(blocks):
        bends, across = bends_of(head_samples[v])
        rate = terms[v] + limit_term(
            bends, across, weno_eps * plan.step_h**2, turn_limit, plan.step_h
        )
        rate = rate + drift_term(
            row_samples[v], weno_eps * plan.step_y**2, speeds[v] * trig[1], spreads[1], plan.step_y
        )
        rate = rate + drift_term(
            col_samples[v], weno_eps * plan.step_x**2, speeds[v] * trig[0], spreads[0], plan.step_x
        )
        results.append(block + time_step * jnp.minimum(rate, 0.0))
    return results


def step_kernel(plan, *refs):
    wide = plan.axes["ha"] > 2
    names = ["value", "heads_even"] + (["heads_odd"] if wide else [])
    names += ["ring", "corner_even"] + (["corner_odd"] if wide else [])
    names += ["packed", "cols_even", "cols_odd", "failure", "offset", "out"]
    names += ["f_a", "f_b", "x_a", "x_b", "s_a", "s_b", "x_s", "trig"]
    r = dict(zip(names, refs, strict=True))
    nv, heads, rows, cols = plan.speeds, plan.heads, plan.rows, plan.cols
    heads_odd, corner_odd = r.get("heads_odd"), r.get("corner_odd")
    pace = plan.pace(r["offset"])
    row, col = iota(plan, 0), iota(plan, 1)
    lower = col % SLOT < DEPTH
    row_first = jnp.logical_and(row >= DEPTH, is_first("gy"))
    row_last = jnp.logical_and(row < DEPTH, is_last("gy"))
    col_first = jnp.logical_and(col >= cols // 2, is_first("gx"))
    col_last = jnp.logical_and(col < cols // 2, is_last("gx"))
    f_a, f_b, x_a, x_b = r["f_a"], r["f_b"], r["x_a"], r["x_b"]
    s_a, s_b, x_s = r["s_a"], r["s_b"], r["x_s"]

    cos_lanes = jnp.zeros((rows, cols), jnp.float32)
    sin_lanes = jnp.zeros((rows, cols), jnp.float32)
    for h in range(-2, heads + 2):
        cosine, sine = plan.trig(h)
        r["trig"][0, h + 2] = cosine
        r["trig"][1, h + 2] = sine
        cos_lanes = jnp.where(col // SLOT == h + 2, cosine, cos_lanes)
        sin_lanes = jnp.where(col // SLOT == h + 2, sine, sin_lanes)

    around = []
    for v in range(nv):
        for h in range(-DEPTH, heads + DEPTH):
            f_a[v, h + DEPTH] = head_block(plan, r["value"], r["heads_even"], heads_odd, v, h)
        for h in range(heads):
            f_b[v, h + 2] = r["ring"][v, h]
        for side in range(2):
            tile = r["corner_even"][v, 1 - side]
            if corner_odd is not None:
                tile = by_side("ha", tile, corner_odd[v, 1 - side])[side]
            base = heads + 2 if side else 0
            f_b[v, base] = tile
            f_b[v, base + 1] = pltpu.roll(tile, DEPTH, 0)
        pair = []
        for part in range(2):
            before, after = by_side("gx", r["cols_even"][v, part], r["cols_odd"][v, part])
            pair.append(jnp.where(lower, before, after))
        around.append(pair)
        for h in range(-2, heads + 2):
            slot = h + 2
            ring = pltpu.roll(pair[0], cols - DEPTH - SLOT * slot, 1)
            x_a[v, slot] = clamp_cols(plan, f_a[v, h + DEPTH], ring, col_first, col_last)
        for h in range(heads):
            slot = h + 2
            ring = pltpu.roll(pair[1], cols - DEPTH - SLOT * slot, 1)
            x_b[v, h] = clamp_cols(plan, f_b[v, slot], ring, col_first, col_last)

    def block_step(h, main, ring, row_of, x_of, base, store):
        blocks = [main[v, h + base] for v in range(nv)]
        heads_near = [[main[v, h + base + j] for j in range(-2, 3)] for v in range(nv)]
        rows_near = [
            ring_samples(blocks[v], ring[v, row_of(h)], row, 0, rows) for v in range(nv)
        ]
        cols_near = [ring_samples(blocks[v], x_of(v, h), col, 1, cols) for v in range(nv)]
        trig = (r["trig"][0, h + 2], r["trig"][1, h + 2])
        results = advanced(plan, blocks, rows_near, cols_near, heads_near, pace, trig)
        for v in range(nv):
            store(v, h, results[v])

    def put_a(v, h, block):
        s_a[v, h + 2] = block

    def put_b(v, h, block):
        s_b[v, h] = block

    def first_a(i, carry):
        block_step(i - 2, f_a, f_b, lambda h: h + 2, lambda v, h: x_a[v, h + 2], DEPTH, put_a)
        return carry

    def first_b(h, carry):
        block_step(h, f_b, f_a, lambda h: h + DEPTH, lambda v, h: x_b[v, h], 2, put_b)
        return carry

    lax.fori_loop(0, heads + 4, first_a, 0)
    lax.fori_loop(0, heads, first_b, 0)

    faces = []
    for keep_own in (jnp.logical_not(lower), lower):
        mains = [jnp.where(keep_own, r["packed"][v, 0], around[v][0]) for v in range(nv)]
        rings = [jnp.where(keep_own, r["packed"][v, 1], around[v][1]) for v in range(nv)]
        rows_near = [ring_samples(mains[v], rings[v], row, 0, rows) for v in range(nv)]
        shift = lambda block, lanes: pltpu.roll(block, lanes % cols, 1)
        cols_near = [[shift(mains[v], -j) for j in (-2, -1)] + [mains[v]] for v in range(nv)]
        cols_near = [near + [shift(near[2], -j) for j in (1, 2)] for near in cols_near]
        heads_near = [
            [mains[v] if j == 0 else shift(mains[v], -SLOT * j) for j in range(-2, 3)]
            for v in range(nv)
        ]
        trig = (cos_lanes, sin_lanes)
        faces.append(advanced(plan, mains, rows_near, cols_near, heads_near, pace, trig))

    for v in range(nv):
        both = jnp.where(lower, faces[0][v], faces[1][v])
        for h in range(heads):
            own = s_a[v, h + 2]
            ring = pltpu.roll(both, cols - DEPTH - SLOT * (h + 2), 1)
            x_s[v, h] = clamp_cols(plan, own, ring, col_first, col_last)
            s_b[v, h] = clamp_rows(plan, own, s_b[v, h], row_first, row_last)

    def put_out(v, h, block):
        half = 0.5 * (r["value"][v, h] + block)
        r["out"][v, h] = jnp.minimum(half, r["failure"][h])

    def second(h, carry):
        block_step(h, s_a, s_b, lambda h: h, lambda v, h: x_s[v, h], 2, put_out)
        return carry

    lax.fori_loop(0, heads, second, 0)


def local(plan, value, obstacles, obstacle_slots, horizon, speed_offset):
    nv, heads, rows, cols = value.shape
    wide = plan.axes["ha"] > 2
    tile = (rows, cols)

    def turn_swaps(payload):
        blocks = [swap(payload, "ha", False, True)]
        return blocks + [swap(payload, "ha", True, True)] if wide else blocks

    beside = turn_swaps(value)
    half = (nv, heads // 2) + tile
    even_rows, odd_rows = call(pack_rows, plan, [half, half], [value], "v")
    even_rows = swap(even_rows, "gy", False)
    odd_rows = swap(odd_rows, "gy", True)
    (failure,) = call(
        failure_field,
        plan,
        [(heads,) + tile],
        [obstacles, obstacle_slots, horizon, speed_offset],
        "ssss",
    )
    ring, corner = call(
        unpack_rows, plan, [value.shape, (nv, 2) + tile], [value, even_rows, odd_rows, failure], "vvva"
    )
    corners = turn_swaps(corner)
    pack = pack_cols if wide else pack_cols_narrow
    (packed,) = call(
        pack, plan, [(nv, 2) + tile], [value, *beside, ring], "v" * (2 + len(beside))
    )
    even_cols = swap(packed, "gx", False)
    odd_cols = swap(packed, "gx", True)
    args = [value, *beside, ring, *corners, packed, even_cols, odd_cols, failure]
    scratch = [
        pltpu.VMEM((nv, heads + 2 * DEPTH) + tile, jnp.float32),
        pltpu.VMEM((nv, heads + 4) + tile, jnp.float32),
        pltpu.VMEM((nv, heads + 4) + tile, jnp.float32),
        pltpu.VMEM((nv, heads) + tile, jnp.float32),
        pltpu.VMEM((nv, heads + 4) + tile, jnp.float32),
        pltpu.VMEM((nv, heads) + tile, jnp.float32),
        pltpu.VMEM((nv, heads) + tile, jnp.float32),
        pltpu.SMEM((2, heads + 4), jnp.float32),
    ]
    (out,) = call(
        step_kernel,
        plan,
        [value.shape],
        args + [speed_offset],
        "v" * len(args) + "s",
        scratch,
        flops=100000000,
    )
    return out


def pack_cols_narrow(plan, value, heads_even, ring, packed_out):
    pack_cols(plan, value, heads_even, None, ring, packed_out)


def solution(mesh):
    in_specs = (P(None, "ha", "gy", "gx"), P(), P("ha", None), P(), P())
    out_specs = P(None, "ha", "gy", "gx")

    def body(value, *rest):
        return local(Plan(mesh, value.shape), value, *rest)

    return jax.shard_map(body, mesh=mesh, in_specs=in_specs, out_specs=out_specs, check_vma=False)
```

```python
import functools
import math

import jax
import jax.numpy as jnp
import numpy as np
from jax import lax
from jax.experimental import pallas as pl
from jax.experimental.pallas import tpu as pltpu
from jax.sharding import PartitionSpec as P

GH = 4

cfl_number = 0.75
weno_eps = 1e-06
half_width = 20.0
speed_step = 0.5
turn_limit = 1.0
accel_limit = 4.0
obstacle_speed = 2.0
car_radius = 0.8

DEPTH = 4
SLOT = 2 * DEPTH


class Plan:
    def __init__(self, mesh, shape):
        self.speeds, self.heads, self.rows, self.cols = shape
        self.axes = dict(mesh.shape)
        self.total_heads = self.heads * self.axes["ha"]
        self.step_x = 2.0 * half_width / (self.cols * self.axes["gx"])
        self.step_y = 2.0 * half_width / (self.rows * self.axes["gy"])
        self.step_h = 2.0 * math.pi / self.total_heads
        assert self.rows == 2 * DEPTH and self.heads >= DEPTH and self.heads % GH == 0
        assert SLOT * (self.heads + DEPTH) <= self.cols
        assert all(size % 2 == 0 for size in self.axes.values())
        index = np.arange(self.total_heads, dtype=np.float32)
        angles = index * np.float32(self.step_h) - np.float32(math.pi)
        self.cosines = np.cos(angles.astype(np.float64))
        self.sines = np.sin(angles.astype(np.float64))
        self.most_cos = float(np.max(np.abs(self.cosines)))
        self.most_sin = float(np.max(np.abs(self.sines)))
        self.most_rate = float(
            np.max(np.abs(self.cosines) / self.step_x + np.abs(self.sines) / self.step_y)
        )

    def trig(self, head):
        place = lax.axis_index("ha")
        picked = []
        for table in (self.cosines, self.sines):
            values = [
                float(table[(a * self.heads + head) % self.total_heads])
                for a in range(self.axes["ha"])
            ]
            value = jnp.float32(values[0])
            for a in range(1, len(values)):
                value = jnp.where(place == a, jnp.float32(values[a]), value)
            picked.append(value)
        return picked

    def pace(self, offset_ref):
        base = offset_ref[0].astype(jnp.float32)
        speeds = [speed_step * (base + float(k)) for k in range(self.speeds)]
        top = functools.reduce(jnp.maximum, [jnp.abs(speed) for speed in speeds])
        total = top * self.most_rate + (turn_limit / self.step_h + accel_limit / speed_step)
        time_step = cfl_number / jnp.full((self.rows, self.cols), total, jnp.float32)
        return speeds, (top * self.most_cos, top * self.most_sin), time_step


def swap(payload, axis, odd, wrap=False):
    count = lax.axis_size(axis)
    if axis != "gy" or not odd or wrap:
        first = 1 if odd else 0
        pairs = [(i, (i + 1) % count) for i in range(first, count, 2)]
        return lax.ppermute(payload, axis, pairs + [(j, i) for i, j in pairs])
    pairs = []
    for x in range(lax.axis_size("gx")):
        for y in range(count):
            end = y in (0, count - 1)
            there = (x ^ 1, y) if end else (x, y + 1 if y % 2 else y - 1)
            pairs.append((x * count + y, there[0] * count + there[1]))
    return lax.ppermute(payload, ("gx", axis), pairs)


def by_side(axis, even_block, odd_block):
    is_even = lax.axis_index(axis) % 2 == 0
    return jnp.where(is_even, odd_block, even_block), jnp.where(is_even, even_block, odd_block)


def is_first(axis):
    return lax.axis_index(axis) == 0


def is_last(axis):
    return lax.axis_index(axis) == lax.axis_size(axis) - 1


def call(body, plan, out_shapes, args, specs, scratch=(), flops=1000000):
    space = {"v": pltpu.VMEM, "s": pltpu.SMEM, "a": pl.ANY}
    return pl.pallas_call(
        functools.partial(body, plan),
        out_shape=[jax.ShapeDtypeStruct(shape, jnp.float32) for shape in out_shapes],
        in_specs=[pl.BlockSpec(memory_space=space[s]) for s in specs],
        out_specs=[pl.BlockSpec(memory_space=pltpu.VMEM) for _ in out_shapes],
        scratch_shapes=scratch,
        name=body.__name__,
        cost_estimate=pl.CostEstimate(flops=flops, bytes_accessed=400000, transcendentals=0),
        compiler_params=pltpu.CompilerParams(vmem_limit_bytes=8 * 2**20),
    )(*args)


def iota(plan, dim):
    return lax.broadcasted_iota(jnp.int32, (plan.rows, plan.cols), dim)


def pack_rows(plan, value, even_out, odd_out):
    row = iota(plan, 0)
    is_even = lax.axis_index("gy") % 2 == 0
    for v in range(plan.speeds):
        for pair in range(plan.heads // 2):
            one, two = value[v, 2 * pair], value[v, 2 * pair + 1]
            low = jnp.where(row < DEPTH, one, pltpu.roll(two, DEPTH, 0))
            high = jnp.where(row < DEPTH, pltpu.roll(one, DEPTH, 0), two)
            even_out[v, pair] = jnp.where(is_even, high, low)
            odd_out[v, pair] = jnp.where(is_even, low, high)


def unpack_rows(plan, value, even_in, odd_in, _, ring_out, corner_out):
    row = iota(plan, 0)
    at_first = jnp.logical_and(row >= DEPTH, is_first("gy"))
    at_last = jnp.logical_and(row < DEPTH, is_last("gy"))
    inner = jnp.logical_or(row < 2, row >= plan.rows - 2)
    edge_heads = (0, 1, plan.heads - 2, plan.heads - 1)
    for v in range(plan.speeds):
        kept = {}
        for pair in range(plan.heads // 2):
            before, after = by_side("gy", even_in[v, pair], odd_in[v, pair])
            one = jnp.where(row < DEPTH, after, pltpu.roll(before, DEPTH, 0))
            two = jnp.where(row < DEPTH, pltpu.roll(after, DEPTH, 0), before)
            for h, ring in ((2 * pair, one), (2 * pair + 1, two)):
                ring = clamp_rows(plan, value[v, h], ring, at_first, at_last)
                ring_out[v, h] = ring
                kept[h] = ring
        for side in range(2):
            one, two = kept[edge_heads[2 * side]], kept[edge_heads[2 * side + 1]]
            corner_out[v, side] = jnp.where(inner, one, pltpu.roll(two, DEPTH, 0))


def clamp_rows(plan, own, ring, at_first, at_last):
    shape = (plan.rows, plan.cols)
    ring = jnp.where(at_first, jnp.broadcast_to(own[0:1], shape), ring)
    return jnp.where(at_last, jnp.broadcast_to(own[plan.rows - 1 :], shape), ring)


def pack_cols(plan, value, heads_even, heads_odd, ring, packed_out, even_out, odd_out):
    col = iota(plan, 1)
    lower = col % SLOT < DEPTH
    slot_id = col // SLOT
    is_even = lax.axis_index("gx") % 2 == 0
    for v in range(plan.speeds):
        main = jnp.zeros((plan.rows, plan.cols), jnp.float32)
        for h in range(-2, plan.heads + 2):
            block = head_block(plan, value, heads_even, heads_odd, v, h)
            main = jnp.where(slot_id == h + 2, pltpu.roll(block, DEPTH + SLOT * (h + 2), 1), main)
        outer = jnp.zeros((plan.rows, plan.cols), jnp.float32)
        for h in range(plan.heads):
            moved = pltpu.roll(ring[v, h], DEPTH + SLOT * (h + 2), 1)
            outer = jnp.where(slot_id == h + 2, moved, outer)
        packed_out[v, 0] = main
        packed_out[v, 1] = outer
        last = jnp.where(lower, main, pltpu.roll(outer, DEPTH, 1))
        first = jnp.where(lower, pltpu.roll(main, plan.cols - DEPTH, 1), outer)
        even_out[v] = jnp.where(is_even, last, first)
        odd_out[v] = jnp.where(is_even, first, last)


def head_block(plan, value, heads_even, heads_odd, v, h):
    if 0 <= h < plan.heads:
        return value[v, h]
    source = h % plan.heads
    if heads_odd is None:
        return heads_even[v, source]
    sides = by_side("ha", heads_even[v, source], heads_odd[v, source])
    return sides[0] if h < 0 else sides[1]


def failure_field(plan, obstacles, slots, horizon, offset, failure_out):
    _, _, time_step = plan.pace(offset)
    moment = horizon[0] + time_step
    col = (lax.axis_index("gx") * plan.cols + iota(plan, 1)).astype(jnp.float32)
    row = (lax.axis_index("gy") * plan.rows + iota(plan, 0)).astype(jnp.float32)
    x_cells = (col + 0.5) * plan.step_x - half_width
    y_cells = (row + 0.5) * plan.step_y - half_width
    for group in range(plan.heads // GH):
        angles = [plan.trig(group * GH + g) for g in range(GH)]

        def step(slot, nearest):
            which = slots[group, slot]
            centre_x = half_width * obstacles[0, which]
            centre_y = half_width * obstacles[1, which]
            away_x = x_cells - (centre_x + moment * (obstacle_speed * obstacles[2, which]))
            away_y = y_cells - (centre_y + moment * (obstacle_speed * obstacles[3, which]))
            reach = 1.25 + 0.75 * obstacles[4, which] + car_radius
            middle = away_x * away_x + away_y * away_y
            updated = []
            for g in range(GH):
                cosine, sine = angles[g]
                front_x, front_y = away_x + cosine, away_y + sine
                back_x, back_y = away_x - cosine, away_y - sine
                squared = jnp.minimum(
                    middle,
                    jnp.minimum(
                        front_x * front_x + front_y * front_y, back_x * back_x + back_y * back_y
                    ),
                )
                updated.append(jnp.minimum(nearest[g], jnp.sqrt(squared) - reach))
            return tuple(updated)

        far = jnp.full((plan.rows, plan.cols), 1e30, jnp.float32)
        nearest = lax.fori_loop(0, slots.shape[1], step, (far,) * GH, unroll=2)
        for g in range(GH):
            failure_out[group * GH + g] = nearest[g]


def sharp(bend, floor):
    t = bend * bend + floor
    return t * t


def sides_of(bends, weights):
    half = 0.5 * weights[1]
    low = half + weights[0]
    high = half + weights[2]
    return (bends[0] - bends[1]) * high, (bends[2] - bends[1]) * low, half / (low * high)


def drift_term(across, bends, weights, drift, spread, spacing):
    a, b, r = sides_of(bends, weights)
    quarter = 0.25 / spacing
    return (drift * (0.5 / spacing)) * across + r * (
        ((spread + drift) * quarter) * a + ((spread - drift) * quarter) * b
    )


def limit_term(across, bends, weights, limit, spacing):
    a, b, r = sides_of(bends, weights)
    r = r * (0.25 * limit / spacing)
    return jnp.abs((0.5 * limit / spacing) * across + r * (a - b)) + r * (a + b)


def bend_of(before, here, after):
    return (after - here) - (here - before)


def stencil(samples, floor):
    bends = [bend_of(*samples[i : i + 3]) for i in range(3)]
    return samples[3] - samples[1], bends, [sharp(bend, floor) for bend in bends]


class Shifts:
    def __init__(self, plan, axis):
        self.axis = axis
        self.length = (plan.rows, plan.cols)[axis]
        place = iota(plan, axis)
        self.ends = {-1: place >= self.length - 1, -2: place >= self.length - 2}
        self.ends.update({1: place < 1, 2: place < 2})

    def at(self, block, ring, offset):
        merged = jnp.where(self.ends[offset], ring, block)
        return pltpu.roll(merged, -offset % self.length, self.axis)

    def both(self, block, ring):
        return self.at(block, ring, -1), self.at(block, ring, 1)

    def samples(self, block, ring):
        return [block if j == 0 else self.at(block, ring, j) for j in range(-2, 3)]

    def turned(self, block, stride=1):
        shift = lambda j: pltpu.roll(block, -stride * j % self.length, self.axis)
        return [block if j == 0 else shift(j) for j in range(-2, 3)]

    def near(self, block, ring, floor):
        before, after = self.both(block, ring)
        bend = bend_of(before, block, after)
        return after - before, bend, sharp(bend, floor)

    def stencil(self, near, ring_bend, ring_weight):
        across, bend, weight = near
        bends = self.both(bend, ring_bend)
        weights = self.both(weight, ring_weight)
        return across, [bends[0], bend, bends[1]], [weights[0], weight, weights[1]]


def speed_terms(blocks):
    floor = weno_eps * speed_step * speed_step
    count = len(blocks)
    at = lambda k: blocks[min(max(k, 0), count - 1)]
    zero = jnp.zeros_like(blocks[0])
    bends = [bend_of(at(k - 1), at(k), at(k + 1)) for k in range(count)]
    weights = [sharp(bend, floor) for bend in bends]
    bends = [zero] + bends + [zero]
    weights = [zero + floor * floor] + weights + [zero + floor * floor]
    return [
        limit_term(
            at(k + 1) - at(k - 1), bends[k : k + 3], weights[k : k + 3], accel_limit, speed_step
        )
        for k in range(count)
    ]


class Terms:
    def __init__(self, plan, offset, trig):
        self.plan, self.trig = plan, trig
        self.speeds, self.spreads, self.time_step = plan.pace(offset)
        self.floor_x = weno_eps * plan.step_x**2
        self.floor_y = weno_eps * plan.step_y**2
        self.floor_h = weno_eps * plan.step_h**2

    def set_trig(self):
        for h in range(-2, self.plan.heads + 2):
            self.trig[0, h + 2], self.trig[1, h + 2] = self.plan.trig(h)

    def x(self, v, h, parts, cosine=None):
        cosine = self.trig[0, h + 2] if cosine is None else cosine
        return drift_term(*parts, self.speeds[v] * cosine, self.spreads[0], self.plan.step_x)

    def y(self, v, h, parts, sine=None):
        sine = self.trig[1, h + 2] if sine is None else sine
        return drift_term(*parts, self.speeds[v] * sine, self.spreads[1], self.plan.step_y)

    def heading(self, parts):
        return limit_term(*parts, turn_limit, self.plan.step_h)

    def heading_of(self, main, v, at):
        blocks, bends, weights = main
        return self.heading((
            blocks[v, at + 1] - blocks[v, at - 1],
            [bends[v, at + j] for j in (-1, 0, 1)],
            [weights[v, at + j] for j in (-1, 0, 1)],
        ))

    def keep_bends(self, blocks, bends, weights, at, v):
        bend = bend_of(blocks[v, at - 1], blocks[v, at], blocks[v, at + 1])
        bends[v, at] = bend
        weights[v, at] = sharp(bend, self.floor_h)

    def step(self, block, rate):
        return block + self.time_step * jnp.minimum(rate, 0.0)


def early_kernel(plan, *refs):
    wide = plan.axes["ha"] > 2
    names = ["value", "heads_even"] + (["heads_odd"] if wide else []) + ["ring", "offset"]
    names += ["blocks", "rate_a", "rate_b", "bends", "weights", "trig"]
    r = dict(zip(names, refs, strict=True))
    nv, heads = plan.speeds, plan.heads
    terms = Terms(plan, r["offset"], r["trig"])
    terms.set_trig()
    rows, columns = Shifts(plan, 0), Shifts(plan, 1)
    blocks, ring = r["blocks"], r["ring"]
    edge = edge_columns(plan)

    def x_term(v, h, block):
        term = terms.x(v, h, stencil(columns.turned(block), terms.floor_x))
        return jnp.where(edge, 0.0, term)

    for v in range(nv):
        for h in range(-DEPTH, heads + DEPTH):
            blocks[v, h + DEPTH] = head_block(
                plan, r["value"], r["heads_even"], r.get("heads_odd"), v, h
            )
    kept = (blocks, r["bends"], r["weights"])

    def bend_step(i, carry):
        for v in range(nv):
            terms.keep_bends(*kept, i, v)
        return carry

    lax.fori_loop(1, heads + 2 * DEPTH - 1, bend_step, 0)

    def own_step(h, inner):
        here = [blocks[v, h + DEPTH] for v in range(nv)]
        outer = [ring[v, h] for v in range(nv)]
        sums = [a + terms.heading_of(kept, v, h + DEPTH) for v, a in enumerate(speed_terms(here))]
        outer_sums = speed_terms(outer)
        for v in range(nv):
            near = rows.near(here[v], outer[v], terms.floor_y)
            outer_near = rows.near(outer[v], here[v], terms.floor_y)
            parts = rows.stencil(near, *outer_near[1:])
            outer_parts = rows.stencil(outer_near, *near[1:])
            r["rate_a"][v, h + 2] = sums[v] + terms.y(v, h, parts) + x_term(v, h, here[v])
            rate = outer_sums[v] + terms.y(v, h, outer_parts) + x_term(v, h, outer[v])
            if inner:
                samples = [ring[v, h + j] for j in range(-2, 3)]
                rate = rate + terms.heading(stencil(samples, terms.floor_h))
            r["rate_b"][v, h] = rate

    def inner_step(h, carry):
        own_step(h, True)
        return carry

    def outer_step(i, carry):
        own_step(edge_of(plan, i, 0), False)
        return carry

    def face_step(i, carry):
        h = edge_of(plan, i, 2)
        here = [blocks[v, h + DEPTH] for v in range(nv)]
        for v, term in enumerate(speed_terms(here)):
            rate = term + terms.heading_of(kept, v, h + DEPTH)
            r["rate_a"][v, h + 2] = rate + x_term(v, h, here[v])
        return carry

    lax.fori_loop(2, heads - 2, inner_step, 0)
    lax.fori_loop(0, 4, outer_step, 0)
    lax.fori_loop(0, 4, face_step, 0)


def edge_columns(plan):
    col = iota(plan, 1)
    return jnp.logical_or(col < 2, col >= plan.cols - 2)


def edge_of(plan, i, out):
    return jnp.where(i < 2, i - out, plan.heads - 4 + i + out)


def late_kernel(plan, *refs):
    wide = plan.axes["ha"] > 2
    names = ["blocks", "ring", "rate_a", "rate_b", "corner_even"]
    names += (["corner_odd"] if wide else []) + ["packed", "cols_even", "cols_odd", "failure"]
    names += ["offset", "out", "f_b", "s_a", "s_b", "x_s", "bends", "weights", "trig"]
    r = dict(zip(names, refs, strict=True))
    nv, heads, cols = plan.speeds, plan.heads, plan.cols
    terms = Terms(plan, r["offset"], r["trig"])
    terms.set_trig()
    rows, columns = Shifts(plan, 0), Shifts(plan, 1)
    row, col = iota(plan, 0), iota(plan, 1)
    blocks, f_b, s_a, s_b, x_s = r["blocks"], r["f_b"], r["s_a"], r["s_b"], r["x_s"]
    edge_terms = {}
    place = col % SLOT
    lower = place < DEPTH
    beyond = jnp.logical_or(
        jnp.logical_and(lower, is_first("gx")),
        jnp.logical_and(jnp.logical_not(lower), is_last("gx")),
    )
    row_first = jnp.logical_and(row >= DEPTH, is_first("gy"))
    row_last = jnp.logical_and(row < DEPTH, is_last("gy"))
    shift = lambda block, lanes: pltpu.roll(block, lanes % cols, 1)

    def clamped(around, own):
        near = jnp.where(place == 3, shift(own, -1), shift(own, -2))
        far = jnp.where(place == 4, shift(own, 1), shift(own, 2))
        return jnp.where(beyond, jnp.where(lower, near, far), around)

    def faces_of(around, own):
        return jnp.where(lower, around, own), jnp.where(lower, own, around)

    def turned(packed, h):
        return pltpu.roll(packed, cols - DEPTH - SLOT * (h + 2), 1)

    edge = edge_columns(plan)

    def edge_term(v, h, part):
        return jnp.where(edge, turned(edge_terms[v, part], h), 0.0)

    cos_lanes = jnp.zeros((plan.rows, cols), jnp.float32)
    sin_lanes = jnp.zeros((plan.rows, cols), jnp.float32)
    for h in range(-2, heads + 2):
        cos_lanes = jnp.where(col // SLOT == h + 2, terms.trig[0, h + 2], cos_lanes)
        sin_lanes = jnp.where(col // SLOT == h + 2, terms.trig[1, h + 2], sin_lanes)

    is_even = lax.axis_index("gx") % 2 == 0
    faces = [[], []]
    for v in range(nv):
        for h in range(heads):
            f_b[v, h + 2] = r["ring"][v, h]
        for side in range(2):
            tile = r["corner_even"][v, 1 - side]
            if wide:
                tile = by_side("ha", tile, r["corner_odd"][v, 1 - side])[side]
            base = heads + 2 if side else 0
            f_b[v, base] = tile
            f_b[v, base + 1] = pltpu.roll(tile, DEPTH, 0)
        even, odd = r["cols_even"][v], r["cols_odd"][v]
        before, after = jnp.where(is_even, odd, even), jnp.where(is_even, even, odd)
        main = jnp.where(lower, before, shift(after, DEPTH))
        outer = jnp.where(lower, shift(before, -DEPTH), after)
        for part, around in ((0, main), (1, outer)):
            own = r["packed"][v, part]
            pair = faces_of(clamped(around, own), own)
            x_terms = [
                terms.x(v, 0, stencil(columns.turned(face), terms.floor_x), cos_lanes)
                for face in pair
            ]
            edge_terms[v, part] = jnp.where(lower, x_terms[1], x_terms[0])
            for side in range(2):
                faces[side].append((pair[side], x_terms[side]))

    for h in range(-2, heads + 2):
        for v in range(nv):
            block = blocks[v, h + DEPTH]
            rate = r["rate_a"][v, h + 2] + edge_term(v, h, 0)
            if not 0 <= h < heads:
                samples = rows.samples(block, f_b[v, h + 2])
                rate = rate + terms.y(v, h, stencil(samples, terms.floor_y))
            s_a[v, h + 2] = terms.step(block, rate)
    for h in range(heads):
        for v in range(nv):
            block = f_b[v, h + 2]
            rate = r["rate_b"][v, h] + edge_term(v, h, 1)
            if not 2 <= h < heads - 2:
                samples = [f_b[v, h + 2 + j] for j in range(-2, 3)]
                rate = rate + terms.heading(stencil(samples, terms.floor_h))
            s_b[v, h] = terms.step(block, rate)

    stepped = [[], []]
    for side in range(2):
        mains = [faces[side][2 * v] for v in range(nv)]
        rings = [faces[side][2 * v + 1] for v in range(nv)]
        sums = speed_terms([main for main, _ in mains])
        for v, (block, x_term) in enumerate(mains):
            samples = rows.samples(block, rings[v][0])
            rate = sums[v] + x_term + terms.y(v, 0, stencil(samples, terms.floor_y), sin_lanes)
            samples = columns.turned(block, SLOT)
            rate = rate + terms.heading(stencil(samples, terms.floor_h))
            stepped[side].append(terms.step(block, rate))

    slot_id = col // SLOT
    for v in range(nv):
        own = jnp.zeros((plan.rows, cols), jnp.float32)
        for h in range(heads):
            block = s_a[v, h + 2]
            own = jnp.where(slot_id == h + 2, shift(block, DEPTH + SLOT * (h + 2)), own)
            s_b[v, h] = clamp_rows(plan, block, s_b[v, h], row_first, row_last)
        around = clamped(jnp.where(lower, stepped[0][v], stepped[1][v]), own)
        for h in range(heads):
            x_s[v, h] = turned(around, h)

    kept = (s_a, r["bends"], r["weights"])

    def bend_step(i, carry):
        for v in range(nv):
            terms.keep_bends(*kept, i, v)
        return carry

    lax.fori_loop(1, heads + 3, bend_step, 0)

    def second(h, carry):
        here = [s_a[v, h + 2] for v in range(nv)]
        sums = speed_terms(here)
        for v, block in enumerate(here):
            samples = columns.samples(block, x_s[v, h])
            rate = terms.x(v, h, stencil(samples, terms.floor_x))
            rate = rate + sums[v] + terms.heading_of(kept, v, h + 2)
            samples = rows.samples(block, s_b[v, h])
            rate = rate + terms.y(v, h, stencil(samples, terms.floor_y))
            half = 0.5 * (blocks[v, h + DEPTH] + terms.step(block, rate))
            r["out"][v, h] = jnp.minimum(half, r["failure"][h])
        return carry

    lax.fori_loop(0, heads, second, 0)


def local(plan, value, obstacles, obstacle_slots, horizon, speed_offset):
    nv, heads, rows, cols = value.shape
    wide = plan.axes["ha"] > 2
    tile = (rows, cols)

    def turn_swaps(payload):
        blocks = [swap(payload, "ha", False, True)]
        return blocks + [swap(payload, "ha", True, True)] if wide else blocks

    beside = turn_swaps(value)
    half = (nv, heads // 2) + tile
    even_rows, odd_rows = call(pack_rows, plan, [half, half], [value], "v")
    even_rows = swap(even_rows, "gy", False)
    odd_rows = swap(odd_rows, "gy", True)
    (failure,) = call(
        failure_field,
        plan,
        [(heads,) + tile],
        [obstacles, obstacle_slots, horizon, speed_offset],
        "ssss",
    )
    ring, corner = call(
        unpack_rows, plan, [value.shape, (nv, 2) + tile], [value, even_rows, odd_rows, failure], "vvva"
    )
    corners = turn_swaps(corner)
    pack = pack_cols if wide else pack_cols_narrow
    packed, even_cols, odd_cols = call(
        pack,
        plan,
        [(nv, 2) + tile, (nv,) + tile, (nv,) + tile],
        [value, *beside, ring],
        "v" * (2 + len(beside)),
    )
    even_cols = swap(even_cols, "gx", False)
    odd_cols = swap(odd_cols, "gx", True)
    deep = (nv, heads + 2 * DEPTH) + tile
    edged = (nv, heads + 4) + tile
    memory = lambda shape: pltpu.VMEM(shape, jnp.float32)
    trig = pltpu.SMEM((2, heads + 4), jnp.float32)
    blocks, rate_a, rate_b = call(
        early_kernel,
        plan,
        [deep, edged, value.shape],
        [value, *beside, ring, speed_offset],
        "v" * (2 + len(beside)) + "s",
        [memory(deep), memory(deep), trig],
        flops=50000000,
    )
    args = [blocks, ring, rate_a, rate_b, *corners, packed, even_cols, odd_cols, failure]
    scratch = [memory(edged), memory(edged), memory(value.shape), memory(value.shape)]
    scratch += [memory(edged), memory(edged), trig]
    (out,) = call(
        late_kernel,
        plan,
        [value.shape],
        args + [speed_offset],
        "v" * len(args) + "s",
        scratch,
        flops=100000000,
    )
    return out


def pack_cols_narrow(plan, value, heads_even, *rest):
    pack_cols(plan, value, heads_even, None, *rest)


def solution(mesh):
    in_specs = (P(None, "ha", "gy", "gx"), P(), P("ha", None), P(), P())
    out_specs = P(None, "ha", "gy", "gx")

    def body(value, *rest):
        return local(Plan(mesh, value.shape), value, *rest)

    return jax.shard_map(body, mesh=mesh, in_specs=in_specs, out_specs=out_specs, check_vma=False)
```
